32 devices in a mesh: group: 2 (over y), tm: 4 (over z), mp: 4 (over x, core).
Axes of the slice: x: 2, y: 2, z: 4, core: 2. Of those that a mesh axis runs over, the one named last changes fastest.
Arguments:
- latents: bfloat16 [2, 4, 256, 1536], P('group', 'tm'), parts along dimension 0, may hold values from -6 to 6
- gsd_table: float32 [8, 6, 1536], replicated, may hold values from -3 to 3
- gsd_bucket: int32 [2, 4], P('group', 'tm'), parts along dimension 0, may hold values from 0 to 7
- clearest: int32 [2], P('group'), parts along dimension 0, may hold values from 0 to 3, as said below
- clouds: int32 [2, 4, 256], P('group'), parts along dimension 0, may hold values from 0 to 1
- cross_query: bfloat16 [1536, 1536], P('tm', 'mp'), may hold values from -5 to 5
- cross_pairs: bfloat16 [1536, 2, 1536], P('tm', None, 'mp'), may hold values from -5 to 5
- cross_merge: bfloat16 [1536, 1536], P('mp', 'tm'), may hold values from -0.15625 to 0.15625
- time_triple: bfloat16 [1536, 3, 1536], P('tm', None, 'mp'), may hold values from -5 to 5
- time_merge: bfloat16 [1536, 1536], P('mp', 'tm'), may hold values from -0.15625 to 0.15625
Outputs:
- updated: bfloat16 [2, 4, 256, 1536], P('group', 'tm'), parts along dimension 0
The draws below stay inside these ranges and needn't reach their ends.
There are 2 independent parts, one for each index of `group`. The reference program is written for one: setup_inputs(seed, part) draws one part's arguments, and reference() takes and returns one part's arrays. A program takes and returns all parts, laid end to end along the dimension named above; an argument that names none is the same for every part. Nothing has to cross between parts.
Inputs may be any that keep to these rules, and one draw needn't show every extreme that they name: clearest[s] is one of the stack's dates; that date has no cloudy token, and no date of stack s has fewer cloudy tokens.
All inputs are finite; a program needn't handle non-finite values.
Results may differ from the reference program's by a relative error of at most 0.014.
The reference program's roundings to bfloat16 on the way count: a program that leaves them out, or rounds other values in their place, can miss the bound.
Values may be sent and summed in bfloat16 or wider, within the bound.
A program may use at most 64 MiB of HBM per device.

```python
import jax
import jax.numpy as jnp
from jax import lax

D = 1536
HEADS = 24
HEAD_DIM = 64
BUCKETS = 8
TOKENS = 256
STACKS = 1
DATES = 4
HEAD_GROUPS = 4


def clipped(key, shape):
    return jnp.clip(jax.random.normal(key, shape, jnp.float32), -6.0, 6.0)


def query_key(key, first, second):
    factor = D ** (-0.5)
    base_query = clipped(jax.random.fold_in(key, first), (D, D))
    base_key = clipped(jax.random.fold_in(key, second), (D, D))
    return (base_query * factor, base_key * factor)


def value_part(key, index):
    return clipped(jax.random.fold_in(key, index), (D, D)) * D ** (-0.5)


def draw_cross_query(key, part):
    query_part, key_part = query_key(key, 1, 2)
    return query_part.astype(jnp.bfloat16)


def draw_cross_pairs(key, part):
    query_part, key_part = query_key(key, 1, 2)
    return jnp.stack([key_part, value_part(key, 3)], axis=1).astype(jnp.bfloat16)


def draw_time_triple(key, part):
    query_part, key_part = query_key(key, 4, 5)
    return jnp.stack([query_part, key_part, value_part(key, 6)], axis=1).astype(jnp.bfloat16)


def draw_latents(key, part):
    shape = (STACKS, DATES, TOKENS, D)
    base = clipped(jax.random.fold_in(key, 7), shape)
    return base.astype(jnp.bfloat16)


def cloud_plan(key):
    rate = jax.random.randint(jax.random.fold_in(key, 21), (STACKS, DATES, 1), 0, 9)
    rolled = jax.random.randint(jax.random.fold_in(key, 22), (STACKS, DATES, TOKENS), 0, 16)
    flags = (rolled < rate).astype(jnp.int32)
    counted = jnp.sum(flags, axis=2)
    order = jax.random.permutation(jax.random.fold_in(key, 23), DATES).astype(jnp.int32)
    ranking = counted * DATES + order[None, :]
    chosen = jnp.argsort(ranking, axis=1, stable=True)[:, 0].astype(jnp.int32)
    flags = jnp.where(jnp.arange(DATES)[None, :, None] == chosen[:, None, None], 0, flags)
    return (flags.astype(jnp.int32), chosen)


def draw_clouds(key, part):
    flags, chosen = cloud_plan(key)
    return flags


def draw_clearest(key, part):
    flags, chosen = cloud_plan(key)
    return chosen


def set_ends(array, stream_key, smallest, high):
    dims = array.shape
    place = [jax.random.randint(jax.random.fold_in(stream_key, axis), (), 0, dims[axis]) for axis in range(len(dims))]
    array = array.at[tuple(place)].set(smallest)
    longest = dims.index(max(dims))
    place[longest] = (place[longest] + 1) % dims[longest]
    return array.at[tuple(place)].set(high)


def shard_levels(rng, extent, shards, low, largest):
    loudness, own = 1.0, jax.random.fold_in(rng, 6)
    for dim, shards_of in shards:
        steps = jnp.exp(jax.random.uniform(jax.random.fold_in(own, dim), (shards_of,), jnp.float32, low / len(shards), largest / len(shards)))
        loudness = loudness * jnp.repeat(steps, extent[dim] // shards_of).reshape([-1 if axis == dim else 1 for axis in range(len(extent))])
    return loudness


def centred(stream_key, extent, deviation, reach, pieces=(), held_as=jnp.bfloat16):
    level = shard_levels(stream_key, extent, pieces, -0.22, 0.18) if pieces else 1.0
    entries = jax.random.normal(stream_key, extent, jnp.float32) * deviation * level
    return jnp.minimum(jnp.maximum(entries, -reach), reach).astype(held_as)


def setup_inputs(seed: int = 0, part: int = 0) -> dict:
    key_list = jax.random.split(jax.random.key(seed), 11)
    own_keys = jax.random.split(jax.random.fold_in(key_list[10], part), 11)
    latents = draw_latents(jax.random.fold_in(jax.random.fold_in(key_list[10], part), 71), part)
    gsd_table = centred(key_list[1], (BUCKETS, 6, D), 0.5, 3.0, (), jnp.float32)
    gsd_bucket = set_ends(jax.random.randint(own_keys[2], (STACKS, DATES), 0, BUCKETS), jax.random.fold_in(own_keys[2], 1), 0, BUCKETS - 1).astype(jnp.int32)
    clearest = draw_clearest(jax.random.fold_in(jax.random.fold_in(key_list[10], part), 71), part)
    clouds = draw_clouds(jax.random.fold_in(jax.random.fold_in(key_list[10], part), 71), part)
    cross_query = draw_cross_query(jax.random.fold_in(key_list[10], 71), part)
    cross_pairs = draw_cross_pairs(jax.random.fold_in(key_list[10], 71), part)
    cross_merge = centred(key_list[7], (D, D), D ** -0.5, 0.15625, ((0, 4), (1, 4)))
    time_triple = draw_time_triple(jax.random.fold_in(key_list[10], 71), part)
    time_merge = centred(key_list[9], (D, D), D ** -0.5, 0.15625, ((0, 4), (1, 4)))
    return dict(latents=latents, gsd_table=gsd_table, gsd_bucket=gsd_bucket, clearest=clearest, clouds=clouds, cross_query=cross_query, cross_pairs=cross_pairs, cross_merge=cross_merge, time_triple=time_triple, time_merge=time_merge)


def normalize(values):
    centre = lax.optimization_barrier(jnp.mean(values, axis=-1, keepdims=True))
    shifted = values - centre
    variance = lax.optimization_barrier(jnp.mean(shifted * shifted, axis=-1, keepdims=True))
    return shifted * lax.rsqrt(variance + 1e-06)

def softmax_rows(scores):
    highest = lax.optimization_barrier(jnp.max(scores, axis=-1, keepdims=True))
    weights = jnp.exp(scores - highest)
    return weights / lax.optimization_barrier(jnp.sum(weights, axis=-1, keepdims=True))

def grouped_out(heads_out, weight):
    group_width = heads_out.shape[1] // HEAD_GROUPS
    summed = jnp.zeros((heads_out.shape[0], weight.shape[1]), jnp.float32)
    for member in range(HEAD_GROUPS):
        partial_sum = jnp.dot(heads_out[:, member * group_width:(member + 1) * group_width], weight[member * group_width:(member + 1) * group_width], preferred_element_type=jnp.float32)
        rounded = lax.optimization_barrier(partial_sum.astype(jnp.bfloat16))
        summed = summed + rounded.astype(jnp.float32)
    return summed

def reference(latents, gsd_table, gsd_bucket, clearest, clouds, cross_query, cross_pairs, cross_merge, time_triple, time_merge):
    scale_factor = HEAD_DIM ** (-0.5)
    outputs = []
    for stack_index in range(STACKS):
        values = latents[stack_index].astype(jnp.float32)
        modulation = gsd_table[gsd_bucket[stack_index]][:, :, None, :]
        normed = (normalize(values) * (1.0 + modulation[:, 1]) + modulation[:, 0]).astype(jnp.bfloat16)
        ref_rows = lax.dynamic_index_in_dim(normed, clearest[stack_index], 0, keepdims=False)
        key_value = jnp.dot(ref_rows, cross_pairs.reshape(D, 2 * D), preferred_element_type=jnp.float32).astype(jnp.bfloat16).reshape(TOKENS, 2, HEADS, HEAD_DIM)
        key_rows = key_value[:, 0].astype(jnp.float32)
        value_rows = key_value[:, 1].astype(jnp.float32)
        queries = jnp.dot(normed.reshape(DATES * TOKENS, D), cross_query, preferred_element_type=jnp.float32).astype(jnp.bfloat16).reshape(DATES, TOKENS, HEADS, HEAD_DIM)

        def cross_date(date_queries):
            scores = jnp.einsum('qhe,khe->hqk', date_queries.astype(jnp.float32), key_rows) * scale_factor
            attn_weights = softmax_rows(scores).astype(jnp.bfloat16)
            mixed_out = jnp.einsum('hqk,khe->qhe', attn_weights.astype(jnp.float32), value_rows)
            return mixed_out.astype(jnp.bfloat16).reshape(TOKENS, D)
        attended = lax.map(cross_date, queries)
        cross_sum = grouped_out(attended.reshape(DATES * TOKENS, D), cross_merge).reshape(DATES, TOKENS, D)
        middle = values + modulation[:, 2] * cross_sum
        normed_two = (normalize(middle) * (1.0 + modulation[:, 4]) + modulation[:, 3]).astype(jnp.bfloat16)
        triple = jnp.dot(normed_two.reshape(DATES * TOKENS, D), time_triple.reshape(D, 3 * D), preferred_element_type=jnp.float32).astype(jnp.bfloat16).reshape(DATES, TOKENS, 3, HEADS, HEAD_DIM)
        time_queries = triple[:, :, 0].astype(jnp.float32)
        time_keys = triple[:, :, 1].astype(jnp.float32)
        time_values = triple[:, :, 2].astype(jnp.float32)
        scores_time = jnp.einsum('dlhe,flhe->lhdf', time_queries, time_keys) * scale_factor
        allowed = jnp.transpose(clouds[stack_index] == 0, (1, 0))
        scores_time = jnp.where(allowed[:, None, None, :], scores_time, -1e+30)
        time_weights = softmax_rows(scores_time).astype(jnp.bfloat16)
        time_attended = jnp.einsum('lhdf,flhe->dlhe', time_weights.astype(jnp.float32), time_values).astype(jnp.bfloat16).reshape(DATES * TOKENS, D)
        time_sum = grouped_out(time_attended, time_merge).reshape(DATES, TOKENS, D)
        outputs.append((middle + modulation[:, 5] * time_sum).astype(jnp.bfloat16))
    return jnp.stack(outputs)
```

```python
import functools

import jax
import jax.numpy as jnp
from jax import lax
from jax.experimental import pallas as pl
from jax.experimental.pallas import tpu as pltpu
from jax.sharding import PartitionSpec as P

HEAD_DIM = 64


def broadcast(block, axis, holder):
    block = jnp.where(lax.axis_index(axis) == holder, block, jnp.zeros_like(block))
    return lax.psum(block, axis)


def normalize(values):
    centre = jnp.mean(values, axis=-1, keepdims=True)
    shifted = values - centre
    variance = jnp.mean(shifted * shifted, axis=-1, keepdims=True)
    return shifted * lax.rsqrt(variance + 1e-06)


def softmax_rows(scores):
    highest = jnp.max(scores, axis=-1, keepdims=True)
    weights = jnp.exp(scores - highest)
    return weights / jnp.sum(weights, axis=-1, keepdims=True)


def shards(
    latents,
    gsd_table,
    gsd_bucket,
    clearest,
    clouds,
    cross_query,
    cross_pairs,
    cross_merge,
    time_triple,
    time_merge,
):
    stacks = latents.shape[0]
    seq_tokens = latents.shape[2]
    model_width = latents.shape[3]
    local_width = cross_query.shape[1]
    local_heads = local_width // HEAD_DIM
    buckets = gsd_table.shape[0]
    scale_factor = HEAD_DIM ** (-0.5)
    my_buckets = gsd_bucket.reshape(stacks)
    one_hot = (my_buckets[:, None] == jnp.arange(buckets, dtype=jnp.int32)[None, :]).astype(
        jnp.float32
    )
    modulation = jnp.dot(
        one_hot, gsd_table.reshape(buckets, 6 * model_width), precision=lax.Precision.HIGHEST
    ).reshape(stacks, 6, 1, 1, model_width)
    values = latents.astype(jnp.float32)
    normed = (normalize(values) * (1.0 + modulation[:, 1]) + modulation[:, 0]).astype(jnp.bfloat16)
    full_query, full_pairs, full_merge, full_triple, full_time = (
        lax.all_gather(cross_query, "tm", axis=0, tiled=True),
        lax.all_gather(cross_pairs, "tm", axis=0, tiled=True),
        lax.all_gather(cross_merge, "tm", axis=1, tiled=True),
        lax.all_gather(time_triple, "tm", axis=0, tiled=True),
        lax.all_gather(time_merge, "tm", axis=1, tiled=True),
    )
    flat_rows = normed.reshape(stacks * seq_tokens, model_width)
    queries = jnp.dot(flat_rows, full_query, preferred_element_type=jnp.float32).astype(
        jnp.bfloat16
    )

    def project_reference(ref_rows):
        return jnp.einsum(
            "ld,dce->lce", ref_rows, full_pairs, preferred_element_type=jnp.float32
        ).astype(jnp.bfloat16)

    def empty_pairs(ref_rows):
        return jnp.zeros((ref_rows.shape[0], 2, local_width), jnp.bfloat16)

    position = lax.axis_index("tm")
    owner_date = clearest[0]
    local_pair = lax.cond(position == owner_date, project_reference, empty_pairs, normed[0, 0])
    key_pair = broadcast(local_pair, "tm", owner_date)
    pair_list = [key_pair]
    key_pairs = jnp.stack(pair_list)
    heads_query = queries.reshape(stacks, seq_tokens, local_heads, HEAD_DIM)
    heads_key = key_pairs[:, :, 0].reshape(stacks, seq_tokens, local_heads, HEAD_DIM)
    heads_value = key_pairs[:, :, 1].reshape(stacks, seq_tokens, local_heads, HEAD_DIM)
    scores = (
        jnp.einsum("sqhe,skhe->shqk", heads_query, heads_key, preferred_element_type=jnp.float32)
        * scale_factor
    )
    attn_weights = softmax_rows(scores).astype(jnp.bfloat16)
    attended = jnp.einsum(
        "shqk,skhe->sqhe", attn_weights, heads_value, preferred_element_type=jnp.float32
    ).astype(jnp.bfloat16)
    cross_terms = jnp.dot(
        attended.reshape(stacks * seq_tokens, local_width),
        full_merge,
        preferred_element_type=jnp.float32,
    )
    cross_sum = lax.psum(cross_terms.astype(jnp.bfloat16), "mp").astype(jnp.float32)
    middle = values + modulation[:, 2] * cross_sum.reshape(stacks, 1, seq_tokens, model_width)
    normed_two = (normalize(middle) * (1.0 + modulation[:, 4]) + modulation[:, 3]).astype(
        jnp.bfloat16
    )
    triple = jnp.einsum(
        "nd,dce->nce",
        normed_two.reshape(stacks * seq_tokens, model_width),
        full_triple,
        preferred_element_type=jnp.float32,
    ).astype(jnp.bfloat16)
    triple = triple.reshape(stacks, 1, seq_tokens, 3, local_width)
    patches = lax.all_to_all(triple, "tm", split_axis=2, concat_axis=1, tiled=True)
    date_count = patches.shape[1]
    patch_count = patches.shape[2]
    allowed = lax.dynamic_slice_in_dim(clouds == 0, position * patch_count, patch_count, 2)
    split_heads = patches.reshape(stacks, date_count, patch_count, 3, local_heads, HEAD_DIM)
    scores_time = (
        jnp.einsum(
            "sdphe,sfphe->sphdf",
            split_heads[:, :, :, 0],
            split_heads[:, :, :, 1],
            preferred_element_type=jnp.float32,
        )
        * scale_factor
    )
    visible = jnp.transpose(allowed, (0, 2, 1))[:, :, None, None, :]
    scores_time = jnp.where(visible, scores_time, -1e30)
    time_weights = softmax_rows(scores_time).astype(jnp.bfloat16)
    mixed_out = jnp.einsum(
        "sphdf,sfphe->sdphe",
        time_weights,
        split_heads[:, :, :, 2],
        preferred_element_type=jnp.float32,
    ).astype(jnp.bfloat16)
    mixed_out = mixed_out.reshape(stacks, date_count, patch_count, local_width)
    returned = lax.all_to_all(mixed_out, "tm", split_axis=1, concat_axis=2, tiled=True)
    time_terms = jnp.dot(
        returned.reshape(stacks * seq_tokens, local_width),
        full_time,
        preferred_element_type=jnp.float32,
    )
    time_sum = lax.psum(time_terms.astype(jnp.bfloat16), "mp").astype(jnp.float32)
    return (
        middle + modulation[:, 5] * time_sum.reshape(stacks, 1, seq_tokens, model_width)
    ).astype(jnp.bfloat16)


MESH = pl.DeviceIdType.MESH
UNITS = 8
KEY, VALUE, QUERY, MERGE, TQUERY, TKEY, TVALUE, TMERGE = range(UNITS)
PIECES = ((0, 2), (2, 2), (4, 2), (6, 2))


def block_kernel(
    n_tm,
    n_mp,
    latents,
    table,
    bucket,
    clearest,
    visible,
    shard,
    out,
    weights,
    normed,
    date_rows,
    key_value,
    attended,
    partial,
    gathered,
    middle,
    second,
    triple,
    across,
    mixed,
    returned,
    updated,
    same_head,
    own_sem,
    z_send,
    z_recv,
    y_send,
    y_recv,
    tm_send,
    tm_recv,
    mp_send,
    mp_recv,
):
    f32, bf16 = jnp.float32, jnp.bfloat16
    g, p, m = lax.axis_index("group"), lax.axis_index("tm"), lax.axis_index("mp")
    tokens, width = latents.shape
    depth, local = shard.shape[1], shard.shape[2]
    half = depth // 2
    patch, block = tokens // n_tm, tokens // n_mp
    scale = HEAD_DIM ** (-0.5)

    barrier = pltpu.get_barrier_semaphore()
    for offset in range(1, n_tm):
        pl.semaphore_signal(
            barrier, 1, device_id={"tm": lax.rem(p + offset, n_tm)}, device_id_type=MESH
        )
    for offset in range(1, n_mp):
        pl.semaphore_signal(
            barrier, 1, device_id={"mp": lax.rem(m + offset, n_mp)}, device_id_type=MESH
        )
    pl.semaphore_signal(barrier, 1, device_id={"group": 1 - g}, device_id_type=MESH)
    pl.semaphore_wait(barrier, n_tm + n_mp - 1)

    own = pltpu.make_async_copy(shard, weights.at[:, p], own_sem)
    own.start()
    mine = pl.ds(pl.multiple_of(g * half, 16), half)

    def z_copy(piece, way, step, source, target):
        first, count = PIECES[piece]
        units = pl.ds(first, count)
        slot = weights.at[units, source, mine]
        return pltpu.make_async_remote_copy(
            src_ref=shard.at[units, mine] if step == 0 else slot,
            dst_ref=slot,
            send_sem=z_send.at[piece, way, step],
            recv_sem=z_recv.at[piece, way, step],
            device_id={"tm": target},
            device_id_type=MESH,
        )

    def y_copy(piece, way, step, source):
        first, count = PIECES[piece]
        slot = weights.at[pl.ds(first, count), source, mine]
        return pltpu.make_async_remote_copy(
            src_ref=slot,
            dst_ref=slot,
            send_sem=y_send.at[piece, way, step],
            recv_sem=y_recv.at[piece, way, step],
            device_id={"group": 1 - g},
            device_id_type=MESH,
        )

    def y_arrival(piece, way, step, source):
        first, count = PIECES[piece]
        theirs = pl.ds(pl.multiple_of((1 - g) * half, 16), half)
        slot = weights.at[pl.ds(first, count), source, theirs]
        return pltpu.make_async_remote_copy(
            src_ref=slot,
            dst_ref=slot,
            send_sem=y_send.at[piece, way, step],
            recv_sem=y_recv.at[piece, way, step],
            device_id={"group": 1 - g},
            device_id_type=MESH,
        )

    def sends(piece, step, act):
        @pl.when((p - step >= 0) & (p <= n_tm - 2))
        def _():
            act(z_copy(piece, 0, step, p - step, p + 1))

        @pl.when((p + step <= n_tm - 1) & (p >= 1))
        def _():
            act(z_copy(piece, 1, step, p + step, p - 1))

    def arrivals(piece, step, act):
        @pl.when(p - 1 - step >= 0)
        def _():
            act(0, p - 1 - step)

        @pl.when(p + 1 + step <= n_tm - 1)
        def _():
            act(1, p + 1 + step)

    def send(piece, step):
        sends(piece, step, lambda copy: copy.start())

    def relay(piece, step):
        def act(way, source):
            z_copy(piece, way, step, source, p).wait_recv()
            y_copy(piece, way, step, source).start()

        arrivals(piece, step, act)
        if step + 1 < n_tm - 1:
            send(piece, step + 1)

    def await_piece(piece):
        for step in range(n_tm - 1):
            arrivals(
                piece,
                step,
                lambda way, source: y_arrival(piece, way, step, source).wait_recv(),
            )

    stages = len(PIECES) + n_tm - 1

    def stage(index):
        for piece in range(len(PIECES)):
            step = index - piece
            if 0 <= step < n_tm - 1:
                relay(piece, step)
        if index + 2 < len(PIECES):
            send(index + 2, 0)

    def swap(axis, size, me, sem, source, target):
        send_sem, recv_sem = (tm_send, tm_recv) if axis == "tm" else (mp_send, mp_recv)
        copies = []
        for offset in range(1, size):
            peer = lax.rem(me + offset, size)
            copy = pltpu.make_async_remote_copy(
                src_ref=source(peer),
                dst_ref=target,
                send_sem=send_sem.at[sem, offset - 1],
                recv_sem=recv_sem.at[sem, offset - 1],
                device_id={axis: peer},
                device_id_type=MESH,
            )
            copy.start()
            copies.append(copy)
        return copies

    def finish(copies):
        for copy in copies:
            copy.wait()

    def layer_norm(values):
        centre = jnp.mean(values, axis=-1, keepdims=True)
        shifted = values - centre
        variance = jnp.mean(shifted * shifted, axis=-1, keepdims=True)
        return shifted * lax.rsqrt(variance + 1e-06)

    def project(rows, unit, columns):
        total = None
        for source in range(n_tm):
            term = jnp.dot(
                rows(source * depth), weights[unit, source], preferred_element_type=f32
            )
            total = term if total is None else total + term
        return total.astype(bf16)

    send(0, 0)
    send(1, 0)
    bucket_here = bucket[0]
    shift_a, scale_a = table[bucket_here, 0:1], table[bucket_here, 1:2]

    step_rows = 32

    def first_norm(index, carry):
        rows = pl.ds(pl.multiple_of(index * step_rows, step_rows), step_rows)
        values = latents[rows, :].astype(f32)
        normed[rows, :] = (layer_norm(values) * (1.0 + scale_a) + shift_a).astype(bf16)
        return carry

    lax.fori_loop(0, tokens // step_rows, first_norm, 0)
    date_copies = swap(
        "tm",
        n_tm,
        p,
        0,
        lambda peer: normed.at[pl.ds(pl.multiple_of(peer * patch, 16), patch)],
        date_rows.at[p],
    )
    date_rows[p] = normed[pl.ds(pl.multiple_of(p * patch, 16), patch), :]
    heads_row = lax.broadcasted_iota(jnp.int32, (local, local), 0) >> 6
    heads_column = lax.broadcasted_iota(jnp.int32, (local, local), 1) >> 6
    same_head[...] = jnp.where(heads_row == heads_column, 1.0, 0.0).astype(bf16)
    stage(0)
    stage(1)
    stage(2)
    finish(date_copies)
    own.wait()
    await_piece(0)
    reference_rows = date_rows[clearest[0]]
    for unit in (KEY, VALUE):
        key_value[p, unit] = project(
            lambda start: reference_rows[:, start : start + depth], unit, local
        )
    pair_copies = swap("tm", n_tm, p, 1, lambda peer: key_value.at[p], key_value.at[p])
    stage(3)
    await_piece(1)
    queries = project(lambda start: normed[:, start : start + depth], QUERY, local)
    finish(pair_copies)
    lane = lax.broadcasted_iota(jnp.int32, (1, 2 * HEAD_DIM), 1)
    for pair in range(local // (2 * HEAD_DIM)):
        columns = slice(pair * 2 * HEAD_DIM, (pair + 1) * 2 * HEAD_DIM)
        pair_query = queries[:, columns]
        pair_key = key_value[:, KEY, :, columns].reshape(tokens, 2 * HEAD_DIM)
        pair_value = key_value[:, VALUE, :, columns].reshape(tokens, 2 * HEAD_DIM)
        halves = []
        for member in range(2):
            chosen = (lane >= HEAD_DIM) if member else (lane < HEAD_DIM)
            picked = jnp.where(chosen, pair_query, jnp.zeros_like(pair_query))
            scores = (
                lax.dot_general(
                    picked, pair_key, (((1,), (1,)), ((), ())), preferred_element_type=f32
                )
                * scale
            )
            raised = jnp.exp(scores - jnp.max(scores, axis=-1, keepdims=True))
            probs = (raised / jnp.sum(raised, axis=-1, keepdims=True)).astype(bf16)
            halves.append(jnp.dot(probs, pair_value, preferred_element_type=f32))
        attended[:, columns] = jnp.where(lane < HEAD_DIM, halves[0], halves[1]).astype(bf16)

    def merge(rows, unit, which):
        for source in range(n_tm):
            term = jnp.dot(rows, weights[unit, source], preferred_element_type=f32)
            partial[which, :, :, source * depth : (source + 1) * depth] = term.astype(
                bf16
            ).reshape(n_mp, block, local)
        return swap(
            "mp",
            n_mp,
            m,
            which,
            lambda peer: partial.at[which, peer],
            gathered.at[which, m],
        )

    def merged(which):
        gathered[which, m] = partial[which, m]
        total = gathered[which, 0].astype(f32)
        for source in range(1, n_mp):
            total = total + gathered[which, source].astype(f32)
        return total

    cross_copies = merge(attended[...], MERGE, 0)
    stage(4)
    finish(cross_copies)
    block_rows = pl.ds(pl.multiple_of(m * block, 16), block)
    gate_a = table[bucket_here, 2:3]
    shift_b, scale_b = table[bucket_here, 3:4], table[bucket_here, 4:5]
    middle[...] = latents[block_rows, :].astype(f32) + gate_a * merged(0)
    second[m] = (layer_norm(middle[...]) * (1.0 + scale_b) + shift_b).astype(bf16)
    second_copies = swap("mp", n_mp, m, 2, lambda peer: second.at[m], second.at[m])
    stage(5)
    finish(second_copies)
    triple_copies = []
    for index, unit in enumerate((TQUERY, TKEY, TVALUE)):
        if index == 0:
            await_piece(2)
        if index == 2:
            await_piece(3)
        triple[index] = project(
            lambda start: second[:, :, start : start + depth].reshape(tokens, depth), unit, local
        ).reshape(n_tm, patch, local)
        across[p, index] = triple[index, p]
        triple_copies += swap(
            "tm",
            n_tm,
            p,
            2 + index,
            lambda peer: triple.at[index, peer],
            across.at[p, index],
        )
    finish(triple_copies)
    seen = visible[pl.ds(pl.multiple_of(p * patch, 16), patch), :]
    time_key = across[:, 1].astype(f32)
    for date in range(n_tm):
        products = (across[date, 0].astype(f32)[None] * time_key).reshape(n_tm * patch, local)
        upper = products.astype(bf16)
        lower = (products - upper.astype(f32)).astype(bf16)
        scores = (
            jnp.dot(upper, same_head[...], preferred_element_type=f32)
            + jnp.dot(lower, same_head[...], preferred_element_type=f32)
        ) * scale
        scores = scores.reshape(n_tm, patch, local)
        shown = [
            jnp.where(seen[:, other : other + 1] > 0.5, scores[other], -1e30)
            for other in range(n_tm)
        ]
        highest = functools.reduce(jnp.maximum, shown)
        raised = [jnp.exp(score - highest) for score in shown]
        total = functools.reduce(jnp.add, raised)
        result = None
        for other in range(n_tm):
            prob = (raised[other] / total).astype(bf16).astype(f32)
            term = prob * across[other, 2].astype(f32)
            result = term if result is None else result + term
        mixed[date] = result.astype(bf16)
    mixed_copies = swap("tm", n_tm, p, 5, lambda peer: mixed.at[peer], returned.at[p])
    returned[p] = mixed[p]
    finish(mixed_copies)
    time_copies = merge(returned[...].reshape(tokens, local), TMERGE, 1)
    finish(time_copies)
    gate_b = table[bucket_here, 5:6]
    updated[m] = (middle[...] + gate_b * merged(1)).astype(bf16)
    last_copies = swap("mp", n_mp, m, 3, lambda peer: updated.at[m], updated.at[m])
    finish(last_copies)
    out[...] = updated[...].reshape(tokens, width)

    for piece in range(len(PIECES)):
        for step in range(n_tm - 1):
            sends(piece, step, lambda copy: copy.wait_send())
            arrivals(
                piece,
                step,
                lambda way, source: y_copy(piece, way, step, source).wait_send(),
            )


def fused(
    n_tm,
    n_mp,
    latents,
    gsd_table,
    gsd_bucket,
    clearest,
    clouds,
    cross_query,
    cross_pairs,
    cross_merge,
    time_triple,
    time_merge,
):
    tokens, width = latents.shape[2:]
    depth, local = cross_query.shape
    shard = jnp.stack(
        [
            cross_pairs[:, 0],
            cross_pairs[:, 1],
            cross_query,
            cross_merge,
            time_triple[:, 0],
            time_triple[:, 1],
            time_triple[:, 2],
            time_merge,
        ]
    )
    visible = (clouds[0] == 0).astype(jnp.float32).T
    patch, block = tokens // n_tm, tokens // n_mp
    bf16, f32 = jnp.bfloat16, jnp.float32
    vmem = pl.BlockSpec(memory_space=pltpu.VMEM)
    smem = pl.BlockSpec(memory_space=pltpu.SMEM)
    dma = pltpu.SemaphoreType.DMA
    pieces = len(PIECES)
    result = pl.pallas_call(
        functools.partial(block_kernel, n_tm, n_mp),
        out_shape=jax.ShapeDtypeStruct((tokens, width), bf16),
        in_specs=[vmem, vmem, smem, smem, vmem, pl.BlockSpec(memory_space=pl.ANY)],
        out_specs=vmem,
        scratch_shapes=[
            pltpu.VMEM((UNITS, n_tm, depth, local), bf16),
            pltpu.VMEM((tokens, width), bf16),
            pltpu.VMEM((n_tm, patch, width), bf16),
            pltpu.VMEM((n_tm, 2, patch, local), bf16),
            pltpu.VMEM((tokens, local), bf16),
            pltpu.VMEM((2, n_mp, block, width), bf16),
            pltpu.VMEM((2, n_mp, block, width), bf16),
            pltpu.VMEM((block, width), f32),
            pltpu.VMEM((n_mp, block, width), bf16),
            pltpu.VMEM((3, n_tm, patch, local), bf16),
            pltpu.VMEM((n_tm, 3, patch, local), bf16),
            pltpu.VMEM((n_tm, patch, local), bf16),
            pltpu.VMEM((n_tm, patch, local), bf16),
            pltpu.VMEM((n_mp, block, width), bf16),
            pltpu.VMEM((local, local), bf16),
            dma,
            dma((pieces, 2, n_tm - 1)),
            dma((pieces, 2, n_tm - 1)),
            dma((pieces, 2, n_tm - 1)),
            dma((pieces, 2, n_tm - 1)),
            dma((6, n_tm - 1)),
            dma((6, n_tm - 1)),
            dma((4, n_mp - 1)),
            dma((4, n_mp - 1)),
        ],
        compiler_params=pltpu.CompilerParams(
            collective_id=0, has_side_effects=True, vmem_limit_bytes=56 * 1024 * 1024
        ),
    )(latents[0, 0], gsd_table, gsd_bucket.reshape(1), clearest, visible, shard)
    return result[None, None]


def fits(mesh, latents, cross_query):
    n_tm, n_mp = mesh.shape["tm"], mesh.shape["mp"]
    tokens, width = latents.shape[2:]
    depth, local = width // n_tm, width // n_mp
    return (
        mesh.shape["group"] == 2
        and latents.shape[0] == 2
        and latents.shape[1] == n_tm
        and n_tm <= 8
        and n_mp >= 2
        and tokens % (16 * n_tm) == 0
        and tokens % (16 * n_mp) == 0
        and depth % 128 == 0
        and depth == local
    )


def solution(mesh):
    placed = (
        P("group", "tm", None, None),
        P(),
        P("group", "tm"),
        P("group"),
        P("group", None, None),
        P("tm", "mp"),
        P("tm", None, "mp"),
        P("mp", "tm"),
        P("tm", None, "mp"),
        P("mp", "tm"),
    )

    def run(*args):
        body = shards
        if fits(mesh, args[0], args[5]):
            body = functools.partial(fused, mesh.shape["tm"], mesh.shape["mp"])
        return jax.shard_map(
            body,
            mesh=mesh,
            in_specs=placed,
            out_specs=P("group", "tm", None, None),
            check_vma=False,
        )(*args)

    return run
```

```python
import functools

import jax
import jax.numpy as jnp
from jax import lax
from jax.experimental import pallas as pl
from jax.experimental.pallas import tpu as pltpu
from jax.sharding import PartitionSpec as P

HEAD_DIM = 64


def broadcast(block, axis, holder):
    block = jnp.where(lax.axis_index(axis) == holder, block, jnp.zeros_like(block))
    return lax.psum(block, axis)


def normalize(values):
    centre = jnp.mean(values, axis=-1, keepdims=True)
    shifted = values - centre
    variance = jnp.mean(shifted * shifted, axis=-1, keepdims=True)
    return shifted * lax.rsqrt(variance + 1e-06)


def softmax_rows(scores):
    highest = jnp.max(scores, axis=-1, keepdims=True)
    weights = jnp.exp(scores - highest)
    return weights / jnp.sum(weights, axis=-1, keepdims=True)


def shards(
    latents,
    gsd_table,
    gsd_bucket,
    clearest,
    clouds,
    cross_query,
    cross_pairs,
    cross_merge,
    time_triple,
    time_merge,
):
    stacks = latents.shape[0]
    seq_tokens = latents.shape[2]
    model_width = latents.shape[3]
    local_width = cross_query.shape[1]
    local_heads = local_width // HEAD_DIM
    buckets = gsd_table.shape[0]
    scale_factor = HEAD_DIM ** (-0.5)
    my_buckets = gsd_bucket.reshape(stacks)
    one_hot = (my_buckets[:, None] == jnp.arange(buckets, dtype=jnp.int32)[None, :]).astype(
        jnp.float32
    )
    modulation = jnp.dot(
        one_hot, gsd_table.reshape(buckets, 6 * model_width), precision=lax.Precision.HIGHEST
    ).reshape(stacks, 6, 1, 1, model_width)
    values = latents.astype(jnp.float32)
    normed = (normalize(values) * (1.0 + modulation[:, 1]) + modulation[:, 0]).astype(jnp.bfloat16)
    full_query, full_pairs, full_merge, full_triple, full_time = (
        lax.all_gather(cross_query, "tm", axis=0, tiled=True),
        lax.all_gather(cross_pairs, "tm", axis=0, tiled=True),
        lax.all_gather(cross_merge, "tm", axis=1, tiled=True),
        lax.all_gather(time_triple, "tm", axis=0, tiled=True),
        lax.all_gather(time_merge, "tm", axis=1, tiled=True),
    )
    flat_rows = normed.reshape(stacks * seq_tokens, model_width)
    queries = jnp.dot(flat_rows, full_query, preferred_element_type=jnp.float32).astype(
        jnp.bfloat16
    )

    def project_reference(ref_rows):
        return jnp.einsum(
            "ld,dce->lce", ref_rows, full_pairs, preferred_element_type=jnp.float32
        ).astype(jnp.bfloat16)

    def empty_pairs(ref_rows):
        return jnp.zeros((ref_rows.shape[0], 2, local_width), jnp.bfloat16)

    position = lax.axis_index("tm")
    owner_date = clearest[0]
    local_pair = lax.cond(position == owner_date, project_reference, empty_pairs, normed[0, 0])
    key_pair = broadcast(local_pair, "tm", owner_date)
    pair_list = [key_pair]
    key_pairs = jnp.stack(pair_list)
    heads_query = queries.reshape(stacks, seq_tokens, local_heads, HEAD_DIM)
    heads_key = key_pairs[:, :, 0].reshape(stacks, seq_tokens, local_heads, HEAD_DIM)
    heads_value = key_pairs[:, :, 1].reshape(stacks, seq_tokens, local_heads, HEAD_DIM)
    scores = (
        jnp.einsum("sqhe,skhe->shqk", heads_query, heads_key, preferred_element_type=jnp.float32)
        * scale_factor
    )
    attn_weights = softmax_rows(scores).astype(jnp.bfloat16)
    attended = jnp.einsum(
        "shqk,skhe->sqhe", attn_weights, heads_value, preferred_element_type=jnp.float32
    ).astype(jnp.bfloat16)
    cross_terms = jnp.dot(
        attended.reshape(stacks * seq_tokens, local_width),
        full_merge,
        preferred_element_type=jnp.float32,
    )
    cross_sum = lax.psum(cross_terms.astype(jnp.bfloat16), "mp").astype(jnp.float32)
    middle = values + modulation[:, 2] * cross_sum.reshape(stacks, 1, seq_tokens, model_width)
    normed_two = (normalize(middle) * (1.0 + modulation[:, 4]) + modulation[:, 3]).astype(
        jnp.bfloat16
    )
    triple = jnp.einsum(
        "nd,dce->nce",
        normed_two.reshape(stacks * seq_tokens, model_width),
        full_triple,
        preferred_element_type=jnp.float32,
    ).astype(jnp.bfloat16)
    triple = triple.reshape(stacks, 1, seq_tokens, 3, local_width)
    patches = lax.all_to_all(triple, "tm", split_axis=2, concat_axis=1, tiled=True)
    date_count = patches.shape[1]
    patch_count = patches.shape[2]
    allowed = lax.dynamic_slice_in_dim(clouds == 0, position * patch_count, patch_count, 2)
    split_heads = patches.reshape(stacks, date_count, patch_count, 3, local_heads, HEAD_DIM)
    scores_time = (
        jnp.einsum(
            "sdphe,sfphe->sphdf",
            split_heads[:, :, :, 0],
            split_heads[:, :, :, 1],
            preferred_element_type=jnp.float32,
        )
        * scale_factor
    )
    visible = jnp.transpose(allowed, (0, 2, 1))[:, :, None, None, :]
    scores_time = jnp.where(visible, scores_time, -1e30)
    time_weights = softmax_rows(scores_time).astype(jnp.bfloat16)
    mixed_out = jnp.einsum(
        "sphdf,sfphe->sdphe",
        time_weights,
        split_heads[:, :, :, 2],
        preferred_element_type=jnp.float32,
    ).astype(jnp.bfloat16)
    mixed_out = mixed_out.reshape(stacks, date_count, patch_count, local_width)
    returned = lax.all_to_all(mixed_out, "tm", split_axis=1, concat_axis=2, tiled=True)
    time_terms = jnp.dot(
        returned.reshape(stacks * seq_tokens, local_width),
        full_time,
        preferred_element_type=jnp.float32,
    )
    time_sum = lax.psum(time_terms.astype(jnp.bfloat16), "mp").astype(jnp.float32)
    return (
        middle + modulation[:, 5] * time_sum.reshape(stacks, 1, seq_tokens, model_width)
    ).astype(jnp.bfloat16)


MESH = pl.DeviceIdType.MESH
UNITS = 6
QUERY, MERGE, TQUERY, TKEY, TVALUE, TMERGE = range(UNITS)
KEY, VALUE = 0, 1
PIECES = ((QUERY, 1), (MERGE, 1), (TQUERY, 1), (TKEY, 1), (TVALUE, 1), (TMERGE, 1))
PARTS = 2


def block_kernel(
    n_tm,
    n_mp,
    latents,
    table,
    bucket,
    clearest,
    visible,
    shard,
    pair_shard,
    out,
    weights,
    pair_weights,
    normed,
    date_rows,
    reference_rows,
    pair_partial,
    pair_terms,
    key_value,
    attended,
    partial,
    gathered,
    middle,
    second,
    triple,
    across,
    mixed,
    returned,
    updated,
    same_head,
    own_sem,
    pair_sem,
    z_send,
    z_recv,
    y_send,
    y_recv,
    tm_send,
    tm_recv,
    mp_send,
    mp_recv,
    share_send,
    share_recv,
):
    f32, bf16 = jnp.float32, jnp.bfloat16
    g, p, m = lax.axis_index("group"), lax.axis_index("tm"), lax.axis_index("mp")
    tokens, width = latents.shape
    depth, local = shard.shape[1], shard.shape[2]
    half = depth // 2
    patch, block = tokens // n_tm, tokens // n_mp
    scale = HEAD_DIM ** (-0.5)

    barrier = pltpu.get_barrier_semaphore()
    for offset in range(1, n_tm):
        pl.semaphore_signal(
            barrier, 1, device_id={"tm": lax.rem(p + offset, n_tm)}, device_id_type=MESH
        )
    for offset in range(1, n_mp):
        pl.semaphore_signal(
            barrier, 1, device_id={"mp": lax.rem(m + offset, n_mp)}, device_id_type=MESH
        )
    pl.semaphore_signal(barrier, 1, device_id={"group": 1 - g}, device_id_type=MESH)
    pl.semaphore_wait(barrier, n_tm + n_mp - 1)

    own = pltpu.make_async_copy(shard, weights.at[:, p], own_sem)
    own.start()
    own_pair = pltpu.make_async_copy(pair_shard, pair_weights, pair_sem)
    own_pair.start()
    mine = pl.ds(pl.multiple_of(g * half, 16), half)

    def z_copy(piece, way, step, source, target):
        first, count = PIECES[piece]
        units = pl.ds(first, count)
        slot = weights.at[units, source, mine]
        return pltpu.make_async_remote_copy(
            src_ref=shard.at[units, mine] if step == 0 else slot,
            dst_ref=slot,
            send_sem=z_send.at[piece, way, step],
            recv_sem=z_recv.at[piece, way, step],
            device_id={"tm": target},
            device_id_type=MESH,
        )

    def y_copy(piece, way, step, source):
        first, count = PIECES[piece]
        slot = weights.at[pl.ds(first, count), source, mine]
        return pltpu.make_async_remote_copy(
            src_ref=slot,
            dst_ref=slot,
            send_sem=y_send.at[piece, way, step],
            recv_sem=y_recv.at[piece, way, step],
            device_id={"group": 1 - g},
            device_id_type=MESH,
        )

    def y_arrival(piece, way, step, source):
        first, count = PIECES[piece]
        theirs = pl.ds(pl.multiple_of((1 - g) * half, 16), half)
        slot = weights.at[pl.ds(first, count), source, theirs]
        return pltpu.make_async_remote_copy(
            src_ref=slot,
            dst_ref=slot,
            send_sem=y_send.at[piece, way, step],
            recv_sem=y_recv.at[piece, way, step],
            device_id={"group": 1 - g},
            device_id_type=MESH,
        )

    def sends(piece, step, act):
        @pl.when((p - step >= 0) & (p <= n_tm - 2))
        def _():
            act(z_copy(piece, 0, step, p - step, p + 1))

        @pl.when((p + step <= n_tm - 1) & (p >= 1))
        def _():
            act(z_copy(piece, 1, step, p + step, p - 1))

    def arrivals(piece, step, act):
        @pl.when(p - 1 - step >= 0)
        def _():
            act(0, p - 1 - step)

        @pl.when(p + 1 + step <= n_tm - 1)
        def _():
            act(1, p + 1 + step)

    def send(piece, step):
        sends(piece, step, lambda copy: copy.start())

    def relay(piece, step):
        def act(way, source):
            z_copy(piece, way, step, source, p).wait_recv()
            y_copy(piece, way, step, source).start()

        arrivals(piece, step, act)
        if step + 1 < n_tm - 1:
            send(piece, step + 1)

    def await_piece(piece):
        for step in range(n_tm - 1):
            arrivals(
                piece,
                step,
                lambda way, source: y_arrival(piece, way, step, source).wait_recv(),
            )

    stages = len(PIECES) + n_tm - 1

    def stage(index):
        for piece in range(len(PIECES)):
            step = index - piece
            if 0 <= step < n_tm - 1:
                relay(piece, step)
        if index + 2 < len(PIECES):
            send(index + 2, 0)

    def swap(axis, size, me, sem, source, target):
        send_sem, recv_sem = (tm_send, tm_recv) if axis == "tm" else (mp_send, mp_recv)
        copies = []
        for offset in range(1, size):
            peer = lax.rem(me + offset, size)
            copy = pltpu.make_async_remote_copy(
                src_ref=source(peer),
                dst_ref=target,
                send_sem=send_sem.at[sem, offset - 1],
                recv_sem=recv_sem.at[sem, offset - 1],
                device_id={axis: peer},
                device_id_type=MESH,
            )
            copy.start()
            copies.append(copy)
        return copies

    mate = m + 1 - 2 * lax.rem(m, 2)
    across_x = lax.rem(m + 2, n_mp)

    def share_copy(buffer, which, part, hop, slot, target):
        rows = block // PARTS
        place = buffer.at[slot, pl.ds(part * rows, rows)]
        return pltpu.make_async_remote_copy(
            src_ref=place,
            dst_ref=place,
            send_sem=share_send.at[which, part, hop],
            recv_sem=share_recv.at[which, part, hop],
            device_id={"mp": target},
            device_id_type=MESH,
        )

    def share_start(buffer, which):
        for part in range(PARTS):
            share_copy(buffer, which, part, 0, m, across_x).start()
        for part in range(PARTS):
            share_copy(buffer, which, part, 1, m, mate).start()

    def share_finish(buffer, which):
        for part in range(PARTS):
            share_copy(buffer, which, part, 0, across_x, m).wait_recv()
            share_copy(buffer, which, part, 2, across_x, mate).start()
        for part in range(PARTS):
            share_copy(buffer, which, part, 1, mate, m).wait_recv()
            share_copy(buffer, which, part, 2, lax.rem(mate + 2, n_mp), m).wait_recv()
        for part in range(PARTS):
            share_copy(buffer, which, part, 0, m, across_x).wait_send()
            share_copy(buffer, which, part, 1, m, mate).wait_send()
            share_copy(buffer, which, part, 2, across_x, mate).wait_send()

    def finish(copies):
        for copy in copies:
            copy.wait()

    def layer_norm(values):
        centre = jnp.mean(values, axis=-1, keepdims=True)
        shifted = values - centre
        variance = jnp.mean(shifted * shifted, axis=-1, keepdims=True)
        return shifted * lax.rsqrt(variance + 1e-06)

    def project(rows, unit, columns):
        total = None
        for source in range(n_tm):
            term = jnp.dot(
                rows(source * depth), weights[unit, source], preferred_element_type=f32
            )
            total = term if total is None else total + term
        return total.astype(bf16)

    send(0, 0)
    send(1, 0)
    bucket_here = bucket[0]
    shift_a, scale_a = table[bucket_here, 0:1], table[bucket_here, 1:2]

    step_rows = 32

    def first_norm(index, carry):
        rows = pl.ds(pl.multiple_of(index * step_rows, step_rows), step_rows)
        values = latents[rows, :].astype(f32)
        normed[rows, :] = (layer_norm(values) * (1.0 + scale_a) + shift_a).astype(bf16)
        return carry

    lax.fori_loop(0, tokens // step_rows, first_norm, 0)
    block_rows = pl.ds(pl.multiple_of(m * block, 16), block)
    date_copies = swap(
        "tm",
        n_tm,
        p,
        0,
        lambda peer: normed.at[block_rows, pl.ds(pl.multiple_of(peer * depth, 128), depth)],
        date_rows.at[p],
    )
    date_rows[p] = normed[block_rows, pl.ds(pl.multiple_of(p * depth, 128), depth)]
    heads_row = lax.broadcasted_iota(jnp.int32, (local, local), 0) >> 6
    heads_column = lax.broadcasted_iota(jnp.int32, (local, local), 1) >> 6
    same_head[...] = jnp.where(heads_row == heads_column, 1.0, 0.0).astype(bf16)
    stage(0)
    finish(date_copies)
    reference_rows[m] = date_rows[clearest[0]]
    row_copies = swap(
        "mp", n_mp, m, 2, lambda peer: reference_rows.at[m], reference_rows.at[m]
    )
    stage(1)
    finish(row_copies)
    own_pair.wait()
    for unit in (KEY, VALUE):
        term = jnp.dot(
            reference_rows[...].reshape(tokens, depth),
            pair_weights[unit],
            preferred_element_type=f32,
        )
        pair_partial[:, unit] = term.astype(bf16).reshape(n_tm, patch, local)
    term_copies = swap("tm", n_tm, p, 1, lambda peer: pair_partial.at[peer], pair_terms.at[p])
    pair_terms[p] = pair_partial[p]
    stage(2)
    finish(term_copies)
    pair_total = pair_terms[0].astype(f32)
    for source in range(1, n_tm):
        pair_total = pair_total + pair_terms[source].astype(f32)
    key_value[p] = pair_total.astype(bf16)
    pair_copies = swap("tm", n_tm, p, 2, lambda peer: key_value.at[p], key_value.at[p])
    own.wait()
    await_piece(0)
    queries = project(lambda start: normed[:, start : start + depth], QUERY, local)
    stage(3)
    finish(pair_copies)
    lane = lax.broadcasted_iota(jnp.int32, (1, 2 * HEAD_DIM), 1)
    for pair in range(local // (2 * HEAD_DIM)):
        columns = slice(pair * 2 * HEAD_DIM, (pair + 1) * 2 * HEAD_DIM)
        pair_query = queries[:, columns]
        pair_key = key_value[:, KEY, :, columns].reshape(tokens, 2 * HEAD_DIM)
        pair_value = key_value[:, VALUE, :, columns].reshape(tokens, 2 * HEAD_DIM)
        halves = []
        for member in range(2):
            chosen = (lane >= HEAD_DIM) if member else (lane < HEAD_DIM)
            picked = jnp.where(chosen, pair_query, jnp.zeros_like(pair_query))
            scores = (
                lax.dot_general(
                    picked, pair_key, (((1,), (1,)), ((), ())), preferred_element_type=f32
                )
                * scale
            )
            raised = jnp.exp(scores - jnp.max(scores, axis=-1, keepdims=True))
            probs = (raised / jnp.sum(raised, axis=-1, keepdims=True)).astype(bf16)
            halves.append(jnp.dot(probs, pair_value, preferred_element_type=f32))
        attended[:, columns] = jnp.where(lane < HEAD_DIM, halves[0], halves[1]).astype(bf16)

    def merge(rows, unit, which):
        for source in range(n_tm):
            term = jnp.dot(rows, weights[unit, source], preferred_element_type=f32)
            partial[which, :, :, source * depth : (source + 1) * depth] = term.astype(
                bf16
            ).reshape(n_mp, block, local)
        return swap(
            "mp",
            n_mp,
            m,
            which,
            lambda peer: partial.at[which, peer],
            gathered.at[which, m],
        )

    def merged(which):
        gathered[which, m] = partial[which, m]
        total = gathered[which, 0].astype(f32)
        for source in range(1, n_mp):
            total = total + gathered[which, source].astype(f32)
        return total

    await_piece(1)
    cross_copies = merge(attended[...], MERGE, 0)
    stage(4)
    finish(cross_copies)
    gate_a = table[bucket_here, 2:3]
    shift_b, scale_b = table[bucket_here, 3:4], table[bucket_here, 4:5]
    middle[...] = latents[block_rows, :].astype(f32) + gate_a * merged(0)
    second[m] = (layer_norm(middle[...]) * (1.0 + scale_b) + shift_b).astype(bf16)
    share_start(second, 0)
    stage(5)
    share_finish(second, 0)
    triple_copies = []
    for index, unit in enumerate((TQUERY, TKEY, TVALUE)):
        await_piece(unit)
        triple[index] = project(
            lambda start: second[:, :, start : start + depth].reshape(tokens, depth), unit, local
        ).reshape(n_tm, patch, local)
        across[p, index] = triple[index, p]
        triple_copies += swap(
            "tm",
            n_tm,
            p,
            3 + index,
            lambda peer: triple.at[index, peer],
            across.at[p, index],
        )
        if index < 2:
            stage(6 + index)
    finish(triple_copies)
    seen = visible[pl.ds(pl.multiple_of(p * patch, 16), patch), :]
    time_key = across[:, 1].astype(f32)
    for date in range(n_tm):
        products = (across[date, 0].astype(f32)[None] * time_key).reshape(n_tm * patch, local)
        upper = products.astype(bf16)
        lower = (products - upper.astype(f32)).astype(bf16)
        scores = (
            jnp.dot(upper, same_head[...], preferred_element_type=f32)
            + jnp.dot(lower, same_head[...], preferred_element_type=f32)
        ) * scale
        scores = scores.reshape(n_tm, patch, local)
        shown = [
            jnp.where(seen[:, other : other + 1] > 0.5, scores[other], -1e30)
            for other in range(n_tm)
        ]
        highest = functools.reduce(jnp.maximum, shown)
        raised = [jnp.exp(score - highest) for score in shown]
        total = functools.reduce(jnp.add, raised)
        result = None
        for other in range(n_tm):
            prob = (raised[other] / total).astype(bf16).astype(f32)
            term = prob * across[other, 2].astype(f32)
            result = term if result is None else result + term
        mixed[date] = result.astype(bf16)
    mixed_copies = swap("tm", n_tm, p, 6, lambda peer: mixed.at[peer], returned.at[p])
    returned[p] = mixed[p]
    finish(mixed_copies)
    await_piece(5)
    time_copies = merge(returned[...].reshape(tokens, local), TMERGE, 1)
    finish(time_copies)
    gate_b = table[bucket_here, 5:6]
    updated[m] = (middle[...] + gate_b * merged(1)).astype(bf16)
    share_start(updated, 1)
    share_finish(updated, 1)
    out[...] = updated[...].reshape(tokens, width)

    for piece in range(len(PIECES)):
        for step in range(n_tm - 1):
            sends(piece, step, lambda copy: copy.wait_send())
            arrivals(
                piece,
                step,
                lambda way, source: y_copy(piece, way, step, source).wait_send(),
            )


def fused(
    n_tm,
    n_mp,
    latents,
    gsd_table,
    gsd_bucket,
    clearest,
    clouds,
    cross_query,
    cross_pairs,
    cross_merge,
    time_triple,
    time_merge,
):
    tokens, width = latents.shape[2:]
    depth, local = cross_query.shape
    shard = jnp.stack(
        [
            cross_query,
            cross_merge,
            time_triple[:, 0],
            time_triple[:, 1],
            time_triple[:, 2],
            time_merge,
        ]
    )
    pair_shard = jnp.stack([cross_pairs[:, 0], cross_pairs[:, 1]])
    visible = (clouds[0] == 0).astype(jnp.float32).T
    patch, block = tokens // n_tm, tokens // n_mp
    bf16, f32 = jnp.bfloat16, jnp.float32
    vmem = pl.BlockSpec(memory_space=pltpu.VMEM)
    smem = pl.BlockSpec(memory_space=pltpu.SMEM)
    dma = pltpu.SemaphoreType.DMA
    pieces = len(PIECES)
    result = pl.pallas_call(
        functools.partial(block_kernel, n_tm, n_mp),
        out_shape=jax.ShapeDtypeStruct((tokens, width), bf16),
        in_specs=[vmem, vmem, smem, smem, vmem] + [pl.BlockSpec(memory_space=pl.ANY)] * 2,
        out_specs=vmem,
        scratch_shapes=[
            pltpu.VMEM((UNITS, n_tm, depth, local), bf16),
            pltpu.VMEM((2, depth, local), bf16),
            pltpu.VMEM((tokens, width), bf16),
            pltpu.VMEM((n_tm, block, depth), bf16),
            pltpu.VMEM((n_mp, block, depth), bf16),
            pltpu.VMEM((n_tm, 2, patch, local), bf16),
            pltpu.VMEM((n_tm, 2, patch, local), bf16),
            pltpu.VMEM((n_tm, 2, patch, local), bf16),
            pltpu.VMEM((tokens, local), bf16),
            pltpu.VMEM((2, n_mp, block, width), bf16),
            pltpu.VMEM((2, n_mp, block, width), bf16),
            pltpu.VMEM((block, width), f32),
            pltpu.VMEM((n_mp, block, width), bf16),
            pltpu.VMEM((3, n_tm, patch, local), bf16),
            pltpu.VMEM((n_tm, 3, patch, local), bf16),
            pltpu.VMEM((n_tm, patch, local), bf16),
            pltpu.VMEM((n_tm, patch, local), bf16),
            pltpu.VMEM((n_mp, block, width), bf16),
            pltpu.VMEM((local, local), bf16),
            dma,
            dma,
            dma((pieces, 2, n_tm - 1)),
            dma((pieces, 2, n_tm - 1)),
            dma((pieces, 2, n_tm - 1)),
            dma((pieces, 2, n_tm - 1)),
            dma((7, n_tm - 1)),
            dma((7, n_tm - 1)),
            dma((3, n_mp - 1)),
            dma((3, n_mp - 1)),
            dma((2, PARTS, 3)),
            dma((2, PARTS, 3)),
        ],
        compiler_params=pltpu.CompilerParams(
            collective_id=0, has_side_effects=True, vmem_limit_bytes=56 * 1024 * 1024
        ),
    )(latents[0, 0], gsd_table, gsd_bucket.reshape(1), clearest, visible, shard, pair_shard)
    return result[None, None]


def fits(mesh, latents, cross_query):
    n_tm, n_mp = mesh.shape["tm"], mesh.shape["mp"]
    tokens, width = latents.shape[2:]
    depth, local = width // n_tm, width // n_mp
    return (
        mesh.shape["group"] == 2
        and latents.shape[0] == 2
        and latents.shape[1] == n_tm
        and n_tm <= 8
        and n_mp == 4
        and tokens % (16 * n_tm) == 0
        and tokens % (16 * PARTS * n_mp) == 0
        and depth % 128 == 0
        and depth == local
    )


def solution(mesh):
    placed = (
        P("group", "tm", None, None),
        P(),
        P("group", "tm"),
        P("group"),
        P("group", None, None),
        P("tm", "mp"),
        P("tm", None, "mp"),
        P("mp", "tm"),
        P("tm", None, "mp"),
        P("mp", "tm"),
    )

    def run(*args):
        body = shards
        if fits(mesh, args[0], args[5]):
            body = functools.partial(fused, mesh.shape["tm"], mesh.shape["mp"])
        return jax.shard_map(
            body,
            mesh=mesh,
            in_specs=placed,
            out_specs=P("group", "tm", None, None),
            check_vma=False,
        )(*args)

    return run
```

```python
import functools

import jax
import jax.numpy as jnp
from jax import lax
from jax.experimental import pallas as pl
from jax.experimental.pallas import tpu as pltpu
from jax.sharding import PartitionSpec as P

HEAD_DIM = 64


def broadcast(block, axis, holder):
    block = jnp.where(lax.axis_index(axis) == holder, block, jnp.zeros_like(block))
    return lax.psum(block, axis)


def normalize(values):
    centre = jnp.mean(values, axis=-1, keepdims=True)
    shifted = values - centre
    variance = jnp.mean(shifted * shifted, axis=-1, keepdims=True)
    return shifted * lax.rsqrt(variance + 1e-06)


def softmax_rows(scores):
    highest = jnp.max(scores, axis=-1, keepdims=True)
    weights = jnp.exp(scores - highest)
    return weights / jnp.sum(weights, axis=-1, keepdims=True)


def shards(
    latents,
    gsd_table,
    gsd_bucket,
    clearest,
    clouds,
    cross_query,
    cross_pairs,
    cross_merge,
    time_triple,
    time_merge,
):
    stacks = latents.shape[0]
    seq_tokens = latents.shape[2]
    model_width = latents.shape[3]
    local_width = cross_query.shape[1]
    local_heads = local_width // HEAD_DIM
    buckets = gsd_table.shape[0]
    scale_factor = HEAD_DIM ** (-0.5)
    my_buckets = gsd_bucket.reshape(stacks)
    one_hot = (my_buckets[:, None] == jnp.arange(buckets, dtype=jnp.int32)[None, :]).astype(
        jnp.float32
    )
    modulation = jnp.dot(
        one_hot, gsd_table.reshape(buckets, 6 * model_width), precision=lax.Precision.HIGHEST
    ).reshape(stacks, 6, 1, 1, model_width)
    values = latents.astype(jnp.float32)
    normed = (normalize(values) * (1.0 + modulation[:, 1]) + modulation[:, 0]).astype(jnp.bfloat16)
    full_query, full_pairs, full_merge, full_triple, full_time = (
        lax.all_gather(cross_query, "tm", axis=0, tiled=True),
        lax.all_gather(cross_pairs, "tm", axis=0, tiled=True),
        lax.all_gather(cross_merge, "tm", axis=1, tiled=True),
        lax.all_gather(time_triple, "tm", axis=0, tiled=True),
        lax.all_gather(time_merge, "tm", axis=1, tiled=True),
    )
    flat_rows = normed.reshape(stacks * seq_tokens, model_width)
    queries = jnp.dot(flat_rows, full_query, preferred_element_type=jnp.float32).astype(
        jnp.bfloat16
    )

    def project_reference(ref_rows):
        return jnp.einsum(
            "ld,dce->lce", ref_rows, full_pairs, preferred_element_type=jnp.float32
        ).astype(jnp.bfloat16)

    def empty_pairs(ref_rows):
        return jnp.zeros((ref_rows.shape[0], 2, local_width), jnp.bfloat16)

    position = lax.axis_index("tm")
    owner_date = clearest[0]
    local_pair = lax.cond(position == owner_date, project_reference, empty_pairs, normed[0, 0])
    key_pair = broadcast(local_pair, "tm", owner_date)
    pair_list = [key_pair]
    key_pairs = jnp.stack(pair_list)
    heads_query = queries.reshape(stacks, seq_tokens, local_heads, HEAD_DIM)
    heads_key = key_pairs[:, :, 0].reshape(stacks, seq_tokens, local_heads, HEAD_DIM)
    heads_value = key_pairs[:, :, 1].reshape(stacks, seq_tokens, local_heads, HEAD_DIM)
    scores = (
        jnp.einsum("sqhe,skhe->shqk", heads_query, heads_key, preferred_element_type=jnp.float32)
        * scale_factor
    )
    attn_weights = softmax_rows(scores).astype(jnp.bfloat16)
    attended = jnp.einsum(
        "shqk,skhe->sqhe", attn_weights, heads_value, preferred_element_type=jnp.float32
    ).astype(jnp.bfloat16)
    cross_terms = jnp.dot(
        attended.reshape(stacks * seq_tokens, local_width),
        full_merge,
        preferred_element_type=jnp.float32,
    )
    cross_sum = lax.psum(cross_terms.astype(jnp.bfloat16), "mp").astype(jnp.float32)
    middle = values + modulation[:, 2] * cross_sum.reshape(stacks, 1, seq_tokens, model_width)
    normed_two = (normalize(middle) * (1.0 + modulation[:, 4]) + modulation[:, 3]).astype(
        jnp.bfloat16
    )
    triple = jnp.einsum(
        "nd,dce->nce",
        normed_two.reshape(stacks * seq_tokens, model_width),
        full_triple,
        preferred_element_type=jnp.float32,
    ).astype(jnp.bfloat16)
    triple = triple.reshape(stacks, 1, seq_tokens, 3, local_width)
    patches = lax.all_to_all(triple, "tm", split_axis=2, concat_axis=1, tiled=True)
    date_count = patches.shape[1]
    patch_count = patches.shape[2]
    allowed = lax.dynamic_slice_in_dim(clouds == 0, position * patch_count, patch_count, 2)
    split_heads = patches.reshape(stacks, date_count, patch_count, 3, local_heads, HEAD_DIM)
    scores_time = (
        jnp.einsum(
            "sdphe,sfphe->sphdf",
            split_heads[:, :, :, 0],
            split_heads[:, :, :, 1],
            preferred_element_type=jnp.float32,
        )
        * scale_factor
    )
    visible = jnp.transpose(allowed, (0, 2, 1))[:, :, None, None, :]
    scores_time = jnp.where(visible, scores_time, -1e30)
    time_weights = softmax_rows(scores_time).astype(jnp.bfloat16)
    mixed_out = jnp.einsum(
        "sphdf,sfphe->sdphe",
        time_weights,
        split_heads[:, :, :, 2],
        preferred_element_type=jnp.float32,
    ).astype(jnp.bfloat16)
    mixed_out = mixed_out.reshape(stacks, date_count, patch_count, local_width)
    returned = lax.all_to_all(mixed_out, "tm", split_axis=1, concat_axis=2, tiled=True)
    time_terms = jnp.dot(
        returned.reshape(stacks * seq_tokens, local_width),
        full_time,
        preferred_element_type=jnp.float32,
    )
    time_sum = lax.psum(time_terms.astype(jnp.bfloat16), "mp").astype(jnp.float32)
    return (
        middle + modulation[:, 5] * time_sum.reshape(stacks, 1, seq_tokens, model_width)
    ).astype(jnp.bfloat16)


MESH = pl.DeviceIdType.MESH
UNITS = 6
QUERY, MERGE, TQUERY, TKEY, TVALUE, TMERGE = range(UNITS)
KEY, VALUE = 0, 1
PIECES = (QUERY, MERGE, TQUERY, TKEY, TVALUE, TMERGE)
PARTS = 2


def block_kernel(
    n_tm,
    n_mp,
    latents,
    table,
    bucket,
    clearest,
    clouds,
    query_shard,
    merge_shard,
    triple_shard,
    time_shard,
    pair_shard,
    out,
    weights,
    pair_weights,
    normed,
    date_rows,
    reference_rows,
    pair_partial,
    pair_terms,
    key_value,
    attended,
    partial,
    gathered,
    middle,
    second,
    triple,
    across,
    mixed,
    returned,
    updated,
    same_head,
    own_sem,
    pair_sem,
    z_send,
    z_recv,
    y_send,
    y_recv,
    tm_send,
    tm_recv,
    mp_send,
    mp_recv,
    share_send,
    share_recv,
):
    f32, bf16 = jnp.float32, jnp.bfloat16
    g, p, m = lax.axis_index("group"), lax.axis_index("tm"), lax.axis_index("mp")
    tokens, width = latents.shape
    depth, local = query_shard.shape[0], query_shard.shape[1]
    half = depth // 2
    patch, block = tokens // n_tm, tokens // n_mp
    scale = HEAD_DIM ** (-0.5)

    barrier = pltpu.get_barrier_semaphore()
    for offset in range(1, n_tm):
        pl.semaphore_signal(
            barrier, 1, device_id={"tm": lax.rem(p + offset, n_tm)}, device_id_type=MESH
        )
    for offset in range(1, n_mp):
        pl.semaphore_signal(
            barrier, 1, device_id={"mp": lax.rem(m + offset, n_mp)}, device_id_type=MESH
        )
    pl.semaphore_signal(barrier, 1, device_id={"group": 1 - g}, device_id_type=MESH)
    pl.semaphore_wait(barrier, n_tm + n_mp - 1)

    own_copies = [
        pltpu.make_async_copy(query_shard, weights.at[QUERY, p], own_sem.at[0]),
        pltpu.make_async_copy(merge_shard, weights.at[MERGE, p], own_sem.at[1]),
        pltpu.make_async_copy(triple_shard, weights.at[pl.ds(TQUERY, 3), p], own_sem.at[2]),
        pltpu.make_async_copy(time_shard, weights.at[TMERGE, p], own_sem.at[3]),
    ]
    origins = (
        query_shard,
        merge_shard,
        triple_shard.at[0],
        triple_shard.at[1],
        triple_shard.at[2],
        time_shard,
    )
    own_pair = pltpu.make_async_copy(pair_shard, pair_weights, pair_sem)
    mine = pl.ds(pl.multiple_of(g * half, 16), half)

    def z_copy(piece, way, step, source, target):
        slot = weights.at[PIECES[piece], source, mine]
        return pltpu.make_async_remote_copy(
            src_ref=origins[piece].at[mine] if step == 0 else slot,
            dst_ref=slot,
            send_sem=z_send.at[piece, way, step],
            recv_sem=z_recv.at[piece, way, step],
            device_id={"tm": target},
            device_id_type=MESH,
        )

    def y_copy(piece, way, step, source):
        slot = weights.at[PIECES[piece], source, mine]
        return pltpu.make_async_remote_copy(
            src_ref=slot,
            dst_ref=slot,
            send_sem=y_send.at[piece, way, step],
            recv_sem=y_recv.at[piece, way, step],
            device_id={"group": 1 - g},
            device_id_type=MESH,
        )

    def y_arrival(piece, way, step, source):
        theirs = pl.ds(pl.multiple_of((1 - g) * half, 16), half)
        slot = weights.at[PIECES[piece], source, theirs]
        return pltpu.make_async_remote_copy(
            src_ref=slot,
            dst_ref=slot,
            send_sem=y_send.at[piece, way, step],
            recv_sem=y_recv.at[piece, way, step],
            device_id={"group": 1 - g},
            device_id_type=MESH,
        )

    def sends(piece, step, act):
        @pl.when((p - step >= 0) & (p <= n_tm - 2))
        def _():
            act(z_copy(piece, 0, step, p - step, p + 1))

        @pl.when((p + step <= n_tm - 1) & (p >= 1))
        def _():
            act(z_copy(piece, 1, step, p + step, p - 1))

    def arrivals(piece, step, act):
        @pl.when(p - 1 - step >= 0)
        def _():
            act(0, p - 1 - step)

        @pl.when(p + 1 + step <= n_tm - 1)
        def _():
            act(1, p + 1 + step)

    def send(piece, step):
        sends(piece, step, lambda copy: copy.start())

    def relay(piece, step):
        def act(way, source):
            z_copy(piece, way, step, source, p).wait_recv()
            y_copy(piece, way, step, source).start()

        arrivals(piece, step, act)
        if step + 1 < n_tm - 1:
            send(piece, step + 1)

    def await_piece(piece):
        for step in range(n_tm - 1):
            arrivals(
                piece,
                step,
                lambda way, source: y_arrival(piece, way, step, source).wait_recv(),
            )

    stages = len(PIECES) + n_tm - 1

    def stage(index):
        for piece in range(len(PIECES)):
            step = index - piece
            if 0 <= step < n_tm - 1:
                relay(piece, step)
        if index + 2 < len(PIECES):
            send(index + 2, 0)

    def swap(axis, size, me, sem, source, target):
        send_sem, recv_sem = (tm_send, tm_recv) if axis == "tm" else (mp_send, mp_recv)
        copies = []
        for offset in range(1, size):
            peer = lax.rem(me + offset, size)
            copy = pltpu.make_async_remote_copy(
                src_ref=source(peer),
                dst_ref=target,
                send_sem=send_sem.at[sem, offset - 1],
                recv_sem=recv_sem.at[sem, offset - 1],
                device_id={axis: peer},
                device_id_type=MESH,
            )
            copy.start()
            copies.append(copy)
        return copies

    mate = m + 1 - 2 * lax.rem(m, 2)
    across_x = lax.rem(m + 2, n_mp)

    def share_copy(buffer, which, part, hop, slot, target):
        rows = block // PARTS
        place = buffer.at[slot, pl.ds(part * rows, rows)]
        return pltpu.make_async_remote_copy(
            src_ref=place,
            dst_ref=place,
            send_sem=share_send.at[which, part, hop],
            recv_sem=share_recv.at[which, part, hop],
            device_id={"mp": target},
            device_id_type=MESH,
        )

    def share_start(buffer, which):
        for part in range(PARTS):
            share_copy(buffer, which, part, 0, m, across_x).start()
        for part in range(PARTS):
            share_copy(buffer, which, part, 1, m, mate).start()

    def share_finish(buffer, which):
        for part in range(PARTS):
            share_copy(buffer, which, part, 0, across_x, m).wait_recv()
            share_copy(buffer, which, part, 2, across_x, mate).start()
        for part in range(PARTS):
            share_copy(buffer, which, part, 1, mate, m).wait_recv()
            share_copy(buffer, which, part, 2, lax.rem(mate + 2, n_mp), m).wait_recv()
        for part in range(PARTS):
            share_copy(buffer, which, part, 0, m, across_x).wait_send()
            share_copy(buffer, which, part, 1, m, mate).wait_send()
            share_copy(buffer, which, part, 2, across_x, mate).wait_send()

    def finish(copies):
        for copy in copies:
            copy.wait()

    def layer_norm(values):
        centre = jnp.mean(values, axis=-1, keepdims=True)
        shifted = values - centre
        variance = jnp.mean(shifted * shifted, axis=-1, keepdims=True)
        return shifted * lax.rsqrt(variance + 1e-06)

    def project(rows, unit, columns):
        total = None
        for source in range(n_tm):
            term = jnp.dot(
                rows(source * depth), weights[unit, source], preferred_element_type=f32
            )
            total = term if total is None else total + term
        return total.astype(bf16)

    send(0, 0)
    for copy in own_copies:
        copy.start()
    own_pair.start()
    bucket_here = pl.ds(bucket[0], 1)
    shift_a, scale_a = table[0, bucket_here, :], table[1, bucket_here, :]

    step_rows = 32
    steps, own_steps = tokens // step_rows, block // step_rows

    def first_norm(index, carry):
        start = lax.rem(index + m * own_steps, steps) * step_rows
        rows = pl.ds(pl.multiple_of(start, step_rows), step_rows)
        values = latents[rows, :].astype(f32)
        normed[rows, :] = (layer_norm(values) * (1.0 + scale_a) + shift_a).astype(bf16)
        return carry

    lax.fori_loop(0, own_steps, first_norm, 0)
    block_rows = pl.ds(pl.multiple_of(m * block, 16), block)
    date_copies = swap(
        "tm",
        n_tm,
        p,
        0,
        lambda peer: normed.at[block_rows, pl.ds(pl.multiple_of(peer * depth, 128), depth)],
        date_rows.at[p],
    )
    date_rows[p] = normed[block_rows, pl.ds(pl.multiple_of(p * depth, 128), depth)]
    send(1, 0)
    lax.fori_loop(own_steps, steps, first_norm, 0)
    heads_row = lax.broadcasted_iota(jnp.int32, (local, local), 0) >> 6
    heads_column = lax.broadcasted_iota(jnp.int32, (local, local), 1) >> 6
    same_head[...] = jnp.where(heads_row == heads_column, 1.0, 0.0).astype(bf16)
    finish(date_copies)
    reference_rows[m] = date_rows[clearest[0]]
    row_copies = swap(
        "mp", n_mp, m, 4, lambda peer: reference_rows.at[m], reference_rows.at[m]
    )
    stage(0)
    finish(row_copies)
    own_pair.wait()
    for unit in (KEY, VALUE):
        term = jnp.dot(
            reference_rows[...].reshape(tokens, depth),
            pair_weights[unit],
            preferred_element_type=f32,
        )
        pair_partial[:, unit] = term.astype(bf16).reshape(n_tm, patch, local)
    term_copies = swap("tm", n_tm, p, 1, lambda peer: pair_partial.at[peer], pair_terms.at[p])
    pair_terms[p] = pair_partial[p]
    stage(1)
    finish(term_copies)
    pair_total = pair_terms[0].astype(f32)
    for source in range(1, n_tm):
        pair_total = pair_total + pair_terms[source].astype(f32)
    key_value[p] = pair_total.astype(bf16)
    pair_copies = swap("tm", n_tm, p, 2, lambda peer: key_value.at[p], key_value.at[p])
    stage(2)
    for copy in own_copies:
        copy.wait()
    await_piece(0)
    queries = project(lambda start: normed[:, start : start + depth], QUERY, local)
    stage(3)
    finish(pair_copies)
    lane = lax.broadcasted_iota(jnp.int32, (1, 2 * HEAD_DIM), 1)
    for pair in range(local // (2 * HEAD_DIM)):
        columns = slice(pair * 2 * HEAD_DIM, (pair + 1) * 2 * HEAD_DIM)
        pair_query = queries[:, columns]
        pair_key = key_value[:, KEY, :, columns].reshape(tokens, 2 * HEAD_DIM)
        pair_value = key_value[:, VALUE, :, columns].reshape(tokens, 2 * HEAD_DIM)
        halves = []
        for member in range(2):
            chosen = (lane >= HEAD_DIM) if member else (lane < HEAD_DIM)
            picked = jnp.where(chosen, pair_query, jnp.zeros_like(pair_query))
            scores = (
                lax.dot_general(
                    picked, pair_key, (((1,), (1,)), ((), ())), preferred_element_type=f32
                )
                * scale
            )
            raised = jnp.exp(scores - jnp.max(scores, axis=-1, keepdims=True))
            probs = (raised * (1.0 / jnp.sum(raised, axis=-1, keepdims=True))).astype(bf16)
            halves.append(jnp.dot(probs, pair_value, preferred_element_type=f32))
        attended[:, columns] = jnp.where(lane < HEAD_DIM, halves[0], halves[1]).astype(bf16)

    def merge(rows, unit, which):
        copies = []
        for source in range(n_tm):
            term = jnp.dot(rows, weights[unit, source], preferred_element_type=f32)
            partial[which, :, :, source * depth : (source + 1) * depth] = term.astype(
                bf16
            ).reshape(n_mp, block, local)
            if source % 2 == 1:
                columns = pl.ds((source - 1) * depth, 2 * depth)
                copies += swap(
                    "mp",
                    n_mp,
                    m,
                    2 * which + source // 2,
                    lambda peer: partial.at[which, peer, :, columns],
                    gathered.at[which, m, :, columns],
                )
        return copies

    def merged(which):
        gathered[which, m] = partial[which, m]
        total = gathered[which, 0].astype(f32)
        for source in range(1, n_mp):
            total = total + gathered[which, source].astype(f32)
        return total

    await_piece(1)
    cross_copies = merge(attended[...], MERGE, 0)
    stage(4)
    finish(cross_copies)
    gate_a = table[2, bucket_here, :]
    shift_b, scale_b = table[3, bucket_here, :], table[4, bucket_here, :]
    middle[...] = latents[block_rows, :].astype(f32) + gate_a * merged(0)
    second[m] = (layer_norm(middle[...]) * (1.0 + scale_b) + shift_b).astype(bf16)
    share_start(second, 0)
    stage(5)
    share_finish(second, 0)
    triple_copies = []
    for index, unit in enumerate((TQUERY, TKEY, TVALUE)):
        await_piece(unit)
        triple[index] = project(
            lambda start: second[:, :, start : start + depth].reshape(tokens, depth), unit, local
        ).reshape(n_tm, patch, local)
        across[p, index] = triple[index, p]
        triple_copies += swap(
            "tm",
            n_tm,
            p,
            3 + index,
            lambda peer: triple.at[index, peer],
            across.at[p, index],
        )
        if index < 2:
            stage(6 + index)
    token = lax.broadcasted_iota(jnp.int32, (patch, tokens), 1)
    first = lax.broadcasted_iota(jnp.int32, (patch, tokens), 0) + p * patch
    picker = jnp.where(token == first, 1.0, 0.0).astype(bf16)
    clear = jnp.where(clouds[...] == 0, 1.0, 0.0).astype(bf16)
    seen = lax.dot_general(picker, clear, (((1,), (1,)), ((), ())), preferred_element_type=f32)
    finish(triple_copies)
    time_key = across[:, 1].astype(f32)
    for date in range(n_tm):
        products = (across[date, 0].astype(f32)[None] * time_key).reshape(n_tm * patch, local)
        upper = products.astype(bf16)
        lower = (products - upper.astype(f32)).astype(bf16)
        scores = (
            jnp.dot(upper, same_head[...], preferred_element_type=f32)
            + jnp.dot(lower, same_head[...], preferred_element_type=f32)
        ) * scale
        scores = scores.reshape(n_tm, patch, local)
        shown = [
            jnp.where(seen[:, other : other + 1] > 0.5, scores[other], -1e30)
            for other in range(n_tm)
        ]
        highest = functools.reduce(jnp.maximum, shown)
        raised = [jnp.exp(score - highest) for score in shown]
        inverse = 1.0 / functools.reduce(jnp.add, raised)
        result = None
        for other in range(n_tm):
            prob = (raised[other] * inverse).astype(bf16).astype(f32)
            term = prob * across[other, 2].astype(f32)
            result = term if result is None else result + term
        mixed[date] = result.astype(bf16)
    mixed_copies = swap("tm", n_tm, p, 6, lambda peer: mixed.at[peer], returned.at[p])
    returned[p] = mixed[p]
    finish(mixed_copies)
    await_piece(5)
    time_copies = merge(returned[...].reshape(tokens, local), TMERGE, 1)
    finish(time_copies)
    gate_b = table[5, bucket_here, :]
    updated[m] = (middle[...] + gate_b * merged(1)).astype(bf16)
    share_start(updated, 1)
    share_finish(updated, 1)
    out[...] = updated[...].reshape(tokens, width)

    for piece in range(len(PIECES)):
        for step in range(n_tm - 1):
            sends(piece, step, lambda copy: copy.wait_send())
            arrivals(
                piece,
                step,
                lambda way, source: y_copy(piece, way, step, source).wait_send(),
            )


def fused(
    n_tm,
    n_mp,
    latents,
    gsd_table,
    gsd_bucket,
    clearest,
    clouds,
    cross_query,
    cross_pairs,
    cross_merge,
    time_triple,
    time_merge,
):
    tokens, width = latents.shape[2:]
    depth, local = cross_query.shape
    pair_shard = jnp.stack([cross_pairs[:, 0], cross_pairs[:, 1]])
    patch, block = tokens // n_tm, tokens // n_mp
    bf16, f32 = jnp.bfloat16, jnp.float32
    vmem = pl.BlockSpec(memory_space=pltpu.VMEM)
    smem = pl.BlockSpec(memory_space=pltpu.SMEM)
    dma = pltpu.SemaphoreType.DMA
    pieces = len(PIECES)
    result = pl.pallas_call(
        functools.partial(block_kernel, n_tm, n_mp),
        out_shape=jax.ShapeDtypeStruct((tokens, width), bf16),
        in_specs=[vmem, vmem, smem, smem, vmem] + [pl.BlockSpec(memory_space=pl.ANY)] * 5,
        out_specs=vmem,
        scratch_shapes=[
            pltpu.VMEM((UNITS, n_tm, depth, local), bf16),
            pltpu.VMEM((2, depth, local), bf16),
            pltpu.VMEM((tokens, width), bf16),
            pltpu.VMEM((n_tm, block, depth), bf16),
            pltpu.VMEM((n_mp, block, depth), bf16),
            pltpu.VMEM((n_tm, 2, patch, local), bf16),
            pltpu.VMEM((n_tm, 2, patch, local), bf16),
            pltpu.VMEM((n_tm, 2, patch, local), bf16),
            pltpu.VMEM((tokens, local), bf16),
            pltpu.VMEM((2, n_mp, block, width), bf16),
            pltpu.VMEM((2, n_mp, block, width), bf16),
            pltpu.VMEM((block, width), f32),
            pltpu.VMEM((n_mp, block, width), bf16),
            pltpu.VMEM((3, n_tm, patch, local), bf16),
            pltpu.VMEM((n_tm, 3, patch, local), bf16),
            pltpu.VMEM((n_tm, patch, local), bf16),
            pltpu.VMEM((n_tm, patch, local), bf16),
            pltpu.VMEM((n_mp, block, width), bf16),
            pltpu.VMEM((local, local), bf16),
            dma((4,)),
            dma,
            dma((pieces, 2, n_tm - 1)),
            dma((pieces, 2, n_tm - 1)),
            dma((pieces, 2, n_tm - 1)),
            dma((pieces, 2, n_tm - 1)),
            dma((7, n_tm - 1)),
            dma((7, n_tm - 1)),
            dma((5, n_mp - 1)),
            dma((5, n_mp - 1)),
            dma((2, PARTS, 3)),
            dma((2, PARTS, 3)),
        ],
        compiler_params=pltpu.CompilerParams(
            collective_id=0, has_side_effects=True, vmem_limit_bytes=56 * 1024 * 1024
        ),
    )(
        latents[0, 0],
        gsd_table.transpose(1, 0, 2),
        gsd_bucket.reshape(1),
        clearest,
        clouds[0],
        cross_query,
        cross_merge,
        time_triple.transpose(1, 0, 2),
        time_merge,
        pair_shard,
    )
    return result[None, None]


def fits(mesh, latents, cross_query):
    n_tm, n_mp = mesh.shape["tm"], mesh.shape["mp"]
    tokens, width = latents.shape[2:]
    depth, local = width // n_tm, width // n_mp
    return (
        mesh.shape["group"] == 2
        and latents.shape[0] == 2
        and latents.shape[1] == n_tm
        and n_tm in (2, 4, 8)
        and tokens % 32 == 0
        and (tokens // n_mp) % 32 == 0
        and n_mp == 4
        and tokens % (16 * n_tm) == 0
        and tokens % (16 * PARTS * n_mp) == 0
        and depth % 128 == 0
        and depth == local
    )


def solution(mesh):
    placed = (
        P("group", "tm", None, None),
        P(),
        P("group", "tm"),
        P("group"),
        P("group", None, None),
        P("tm", "mp"),
        P("tm", None, "mp"),
        P("mp", "tm"),
        P("tm", None, "mp"),
        P("mp", "tm"),
    )

    def run(*args):
        body = shards
        if fits(mesh, args[0], args[5]):
            body = functools.partial(fused, mesh.shape["tm"], mesh.shape["mp"])
        return jax.shard_map(
            body,
            mesh=mesh,
            in_specs=placed,
            out_specs=P("group", "tm", None, None),
            check_vma=False,
        )(*args)

    return run
```
